32 devices in a mesh: px: 8 (over y, x, core), py: 4 (over z).
Axes of the slice: x: 2, y: 2, z: 4, core: 2. Of those that a mesh axis runs over, the one named last changes fastest.
Arguments:
- velocity: float32 [3, 128, 64, 128], P(None, 'px', 'py'), may hold values from -2 to 2
- states: float32 [3, 128, 64, 128], P(None, 'px', 'py'), may hold values from -6 to 6
- solution: float32 [3, 128, 64, 128], P(None, 'px', 'py'), may hold values from -6 to 6
- residual: float32 [3, 128, 64, 128], P(None, 'px', 'py'), may hold values from -6 to 6
- direction: float32 [3, 128, 64, 128], P(None, 'px', 'py'), may hold values from -6 to 6
Outputs:
- new_solution: float32 [3, 128, 64, 128], P(None, 'px', 'py')
- new_residual: float32 [3, 128, 64, 128], P(None, 'px', 'py')
- new_direction: float32 [3, 128, 64, 128], P(None, 'px', 'py')
The draws below stay inside these ranges and needn't reach their ends.
All inputs are finite; a program needn't handle non-finite values.
Results may differ from the reference program's by a relative error of at most 0.0001.
Values sent between devices are 32-bit elements; how exact they have to be, the bound alone decides.
A program may use at most 64 MiB of HBM per device.

```python
import jax
import jax.numpy as jnp

NZ = 128
NT = 2
KSWEEP = 4
NX = 128
NY = 64


def levels(stream_key, shape, shards, least, largest):
    level, own = 1.0, jax.random.fold_in(stream_key, 6)
    for dim, blocks in shards:
        steps = jnp.exp(jax.random.uniform(jax.random.fold_in(own, dim), (blocks,), jnp.float32, least / len(shards), largest / len(shards)))
        level = level * jnp.repeat(steps, shape[dim] // blocks).reshape([-1 if axis == dim else 1 for axis in range(len(shape))])
    return level


def bell_draw(rng, extent, deviation, reach, cuts=(), dtype=jnp.bfloat16):
    gain = levels(rng, extent, cuts, -0.22, 0.18) if cuts else 1.0
    values = jax.random.normal(rng, extent, jnp.float32) * deviation * gain
    return jnp.minimum(jnp.maximum(values, -reach), reach).astype(dtype)


def setup_inputs(seed: int = 0) -> dict:
    key_of = jax.random.split(jax.random.key(seed), 6)
    return {
        "velocity": bell_draw(key_of[0], (3, NX, NY, NZ), (0.25 * NT), 2.0, ((1, 8), (2, 4)), jnp.float32),
        "states": bell_draw(key_of[1], (NT + 1, NX, NY, NZ), 1.0, 6.0, ((1, 8), (2, 4)), jnp.float32),
        "solution": bell_draw(key_of[2], (3, NX, NY, NZ), 1.0, 6.0, ((1, 8), (2, 4)), jnp.float32),
        "residual": bell_draw(key_of[3], (3, NX, NY, NZ), 1.0, 6.0, ((1, 8), (2, 4)), jnp.float32),
        "direction": bell_draw(key_of[4], (3, NX, NY, NZ), 1.0, 6.0, ((1, 8), (2, 4)), jnp.float32),
    }


reg_beta = 0.5
reg_gamma = 1.0
coarse_beta = 0.1
coarse_gamma = 0.05
jacobi_weight = 0.8


def central(field, axis):
    return 0.5 * (jnp.roll(field, -1, axis) - jnp.roll(field, 1, axis))


def gradient(field):
    return jnp.stack([central(field, 0), central(field, 1), central(field, 2)])


def advection(velocity, field):
    return jnp.sum(velocity * gradient(field), axis=0)


def divergence(velocity, field):
    return central(field * velocity[0], 0) + central(field * velocity[1], 1) + central(field * velocity[2], 2)


def laplace(field, first):
    total = -6.0 * field
    for axis in range(first, first + 3):
        total = total + jnp.roll(field, 1, axis) + jnp.roll(field, -1, axis)
    return total


def restrict(field):
    comps, sx, sy, sz = field.shape
    return jnp.mean(field.reshape(comps, sx // 4, 4, sy // 4, 4, sz // 4, 4), axis=(2, 4, 6))


def prolong(coarse):
    comps, sx, sy, sz = coarse.shape
    spread = jnp.broadcast_to(coarse[:, :, None, :, None, :, None], (comps, sx, 4, sy, 4, sz, 4))
    return spread.reshape(comps, 4 * sx, 4 * sy, 4 * sz)


def coarse_solve(rhs):
    diag_coarse = 6.0 * coarse_beta + coarse_gamma
    approx = jacobi_weight * rhs / diag_coarse
    for sweep_round in range(KSWEEP - 1):
        applied = -coarse_beta * laplace(approx, 1) + coarse_gamma * approx
        approx = approx + jacobi_weight * (rhs - applied) / diag_coarse
    return approx


def precondition(field):
    return field / (6.0 * reg_beta + reg_gamma) + prolong(coarse_solve(restrict(field)))


def hessian(velocity, states, direction):
    delta = 1.0 / NT
    grads = [gradient(states[moment]) for moment in range(NT + 1)]
    increment = jnp.zeros(states.shape[1:], jnp.float32)
    for moment in range(NT):
        first_rate = -advection(velocity, increment) - jnp.sum(direction * grads[moment], axis=0)
        trial = increment + delta * first_rate
        second_rate = -advection(velocity, trial) - jnp.sum(direction * grads[moment + 1], axis=0)
        increment = increment + 0.5 * delta * (first_rate + second_rate)
    adjoint = -increment
    force = 0.5 * adjoint * grads[NT]
    for moment in range(NT - 1, -1, -1):
        first_rate = divergence(velocity, adjoint)
        trial = adjoint + delta * first_rate
        second_rate = divergence(velocity, trial)
        adjoint = adjoint + 0.5 * delta * (first_rate + second_rate)
        weight = 0.5 if moment == 0 else 1.0
        force = force + weight * adjoint * grads[moment]
    return reg_beta * (-laplace(direction, 1)) + reg_gamma * direction + delta * force


def reference(velocity, states, solution, residual, direction):
    precond = precondition(residual)
    image = hessian(velocity, states, direction)
    rz_old = jnp.sum(residual * precond)
    alpha = rz_old / jnp.sum(direction * image)
    new_solution = solution + alpha * direction
    new_residual = residual - alpha * image
    new_precond = precondition(new_residual)
    rz_new = jnp.sum(new_residual * new_precond)
    new_direction = new_precond + (rz_new / rz_old) * direction
    return new_solution, new_residual, new_direction
```

```python
import functools

import jax
import jax.numpy as jnp
from jax import lax
from jax.experimental import pallas as pl
from jax.experimental.pallas import tpu as pltpu
from jax.sharding import PartitionSpec as P

W = 4
DIRS = ((1, 0), (-1, 0), (0, 1), (0, -1), (1, 1), (1, -1), (-1, 1), (-1, -1))
HI = lax.Precision.HIGHEST
WEIGHT = 0.8 / 0.65


def up(v, axis):
    return pltpu.roll(v, v.shape[axis] - 1, axis)


def down(v, axis):
    return pltpu.roll(v, 1, axis)


def kernel(
    px, py, vel, sta, sol, res, dirn, IMG, PR, o_sc, KEEP,
    F, FV, S, T, U, G, TR, CB, AR,
    loc_sem, h_send, h_recv, s_send, s_recv, u_send, u_recv, c_send, c_recv, a_send, a_recv,
):
    nx, ny, nz = sta.shape[1:]
    ex, ey = nx + 2 * W, ny + 2 * W
    me_x, me_y = lax.axis_index("px"), lax.axis_index("py")

    def at(dx, dy):
        return (lax.rem(me_x + (dx + px), px), lax.rem(me_y + (dy + py), py))

    def mesh_copy(src, dst, s, r, dx, dy):
        return pltpu.make_async_remote_copy(
            src_ref=src, dst_ref=dst, send_sem=s, recv_sem=r,
            device_id=at(dx, dy), device_id_type=pl.DeviceIdType.MESH,
        )

    locals_ = []
    for g, a in enumerate((sta, dirn, vel)):
        locals_.append(
            pltpu.make_async_copy(a, F.at[pl.ds(3 * g, 3), pl.ds(W, nx), pl.ds(0, ny)], loc_sem.at[g])
        )
    for i, a in enumerate((res, dirn, sol)):
        locals_.append(pltpu.make_async_copy(a, KEEP.at[i], loc_sem.at[3 + i]))
    RS = KEEP.at[0]

    barrier = pltpu.get_barrier_semaphore()
    total = px * py

    def peer(d):
        other = lax.rem(me_x * py + me_y + d, total)
        return (other // py, lax.rem(other, py))

    def each_peer(body):
        def run(i, carry):
            body(i + 1)
            return carry

        lax.fori_loop(0, total - 1, run, 0, unroll=total <= 64)

    each_peer(
        lambda d: pl.semaphore_signal(
            barrier, inc=1, device_id=peer(d), device_id_type=pl.DeviceIdType.MESH
        )
    )
    for c in locals_:
        c.start()
    pl.semaphore_wait(barrier, total - 1)

    def x_span(dx, w, k):
        return {
            0: (0, nx, W),
            1: (nx - w - k, w, W - w - k),
            -1: (k, w, W + nx + k),
        }[dx]

    def y_span(dy, w, k):
        return {
            0: (0, ny, 0),
            1: (ny - w - k, w, ny + 2 * W - w - k),
            -1: (k, w, ny + k),
        }[dy]

    def halo(make, send, recv, width, corner, base=0):
        copies = []
        for i, (dx, dy) in enumerate(DIRS):
            if dx and dy:
                if not corner:
                    continue
                wide = (corner, corner)
                start = (0, 0)
            else:
                wide = (width, width)
                start = (base, base)
            sx, lx, tx = x_span(dx, wide[0], start[0])
            sy, ly, ty = y_span(dy, wide[1], start[1])
            src, dst = make((pl.ds(sx, lx), pl.ds(sy, ly)), (pl.ds(tx, lx), pl.ds(ty, ly)))
            copies.append(mesh_copy(src, dst, send.at[i], recv.at[i], dx, dy))
        for c in copies:
            c.start()
        return copies

    def field_halo(g, a, slot, *args):
        return halo(
            lambda src, dst: (a.at[(pl.ds(0, 3),) + src], F.at[(pl.ds(3 * g, 3),) + dst]),
            h_send.at[slot], h_recv.at[slot], *args,
        )

    state_copies = field_halo(0, sta, 0, 1, 0)
    near_copies = field_halo(2, vel, 1, 2, 3)

    row = lambda shape: lax.broadcasted_iota(jnp.int32, shape, 0)
    lane = lambda shape: lax.broadcasted_iota(jnp.int32, shape, 1)
    cz = nz // 4
    cx, cy = nx // 4, ny // 4
    lanes = cy * cz
    n_rows = 6 * cx * ny
    m_shape = (nz, lanes)
    gather_z = (row(m_shape) // 4 == lax.rem(lane(m_shape), cz)).astype(jnp.float32)
    t_shape = (lanes, nz)
    spread_z = (lax.rem(row(t_shape), cz) == lane(t_shape) // 4).astype(jnp.float32)
    k_shape = (n_rows, lanes)
    keep = lax.rem(row(k_shape), ny) // 4 == lane(k_shape) // cz
    r_shape = (cx * 8, n_rows)
    src_c, src_x = lane(r_shape) // (cx * ny), lax.rem(lane(r_shape) // ny, cx)
    gather_y = jnp.where(
        jnp.logical_and(row(r_shape) // 8 == src_x, lax.rem(row(r_shape), 8) == src_c), 1.0 / 64.0, 0.0
    )
    p_shape = (n_rows, cx * 8)
    dst_c, dst_x = row(p_shape) // (cx * ny), lax.rem(row(p_shape) // ny, cx)
    spread_y = jnp.where(
        jnp.logical_and(lane(p_shape) // 8 == dst_x, lax.rem(lane(p_shape), 8) == dst_c), 1.0, 0.0
    )

    def sweep(start, planes, step, body):
        def run(i, carry):
            body(start + i * step)
            return carry

        lax.fori_loop(0, planes // step, run, 0, unroll=True)

    for c in locals_[:2]:
        c.wait()
    for c in state_copies:
        c.wait()

    def sources(x):
        own = pl.ds(x, 2)
        at_x = pl.ds(x - W, 2)
        d = [F[3 + k, own, pl.ds(0, ny)] for k in range(3)]
        for n in range(3):
            f = F[n, own]
            grads = (
                (F[n, pl.ds(x + 1, 2)] - F[n, pl.ds(x - 1, 2)])[:, :ny],
                (up(f, 1) - down(f, 1))[:, :ny],
                (up(f, 2) - down(f, 2))[:, :ny],
            )
            S[n, own, pl.ds(0, ny)] = 0.5 * (d[0] * grads[0] + d[1] * grads[1] + d[2] * grads[2])
            for k in range(3):
                G[3 * n + k, at_x] = grads[k]

    sweep(W, nx, 2, sources)
    source_copies = halo(
        lambda src, dst: (
            S.at[pl.ds(0, 2), pl.ds(W + src[0].start, src[0].size), src[1]],
            S.at[(pl.ds(0, 2),) + dst],
        ),
        s_send, s_recv, 3, 2,
    )
    far_copies = halo(
        lambda src, dst: (
            vel.at[(pl.ds(0, 3),) + src],
            FV.at[pl.ds(0, 3), pl.ds(0, nx), pl.ds(dst[1].start - ny, 2)]
            if dst[1].size == 2
            else F.at[(pl.ds(6, 3),) + dst],
        ),
        h_send.at[2], h_recv.at[2], 2, 0, 2,
    )
    direction_copies = field_halo(1, dirn, 3, 1, 0)

    locals_[3].wait()
    rr = jnp.zeros((ny, nz), jnp.float32)
    for c in range(3):
        for b in range(cx):
            r = RS[c, pl.ds(4 * b, 4)]
            TR[c, b] = jnp.sum(r, axis=0)
            rr = rr + jnp.sum(r * r, axis=0)

    locals_[2].wait()
    for c in near_copies:
        c.wait()
    for c in source_copies:
        c.wait()

    def advect(read, x):
        f = read(x)
        v = [F[6 + k, pl.ds(x, 2)] for k in range(3)]
        return f, 0.5 * (
            v[0] * (read(x + 1) - read(x - 1))
            + v[1] * (up(f, 1) - down(f, 1))
            + v[2] * (up(f, 2) - down(f, 2))
        )

    def forward_one(x):
        f, adv = advect(lambda i: S[0, pl.ds(i, 2)], x)
        at_x = pl.ds(x, 2)
        T[1, at_x] = 0.25 * (0.5 * adv - S[1, at_x] - f)

    def forward_two(x):
        f, adv = advect(lambda i: T[1, pl.ds(i, 2)], x)
        at_x = pl.ds(x, 2)
        first = -(adv + S[1, at_x])
        T[2, at_x] = f + 0.5 * first
        T[3, at_x] = f + 0.25 * first

    def forward_three(x):
        f, adv = advect(lambda i: T[2, pl.ds(i, 2)], x)
        at_x = pl.ds(x, 2)
        U[at_x, pl.ds(0, ny)] = 0.25 * (adv[:, :ny] + S[2, at_x, pl.ds(0, ny)]) - T[3, at_x, pl.ds(0, ny)]

    sweep(2, ex - 4, 2, forward_one)
    sweep(3, ex - 6, 2, forward_two)
    sweep(4, ex - 8, 2, forward_three)

    u_copies = halo(
        lambda src, dst: (U.at[pl.ds(W + src[0].start, src[0].size), src[1]], U.at[dst]),
        u_send, u_recv, W, 3,
    )
    for c in direction_copies:
        c.wait()

    def base(x):
        own = pl.ds(x, 2)
        at_x = pl.ds(x - W, 2)
        adj = 0.125 * U[own, pl.ds(0, ny)]
        for k in range(3):
            f = F[3 + k, own]
            neighbours = (
                F[3 + k, pl.ds(x + 1, 2)] + F[3 + k, pl.ds(x - 1, 2)]
                + up(f, 1) + down(f, 1) + up(f, 2) + down(f, 2)
            )[:, :ny]
            IMG[k, at_x] = 4.0 * f[:, :ny] - 0.5 * neighbours + adj * G[6 + k, at_x]

    sweep(W, nx, 2, base)
    for c in far_copies:
        c.wait()
    tile_row = lax.broadcasted_iota(jnp.int32, (1, 1, 2 * W, nz), 2)
    band, beyond = pl.ds(W, nx), pl.ds(ny, 2 * W)
    from_far = jnp.logical_and(tile_row >= 2, tile_row < 2 * W - 2)
    F[pl.ds(6, 3), band, beyond] = jnp.where(from_far, FV[...], F[pl.ds(6, 3), band, beyond])
    for c in u_copies:
        c.wait()

    def diverge(read, x):
        f = read(x)
        flux_y = f * F[7, pl.ds(x, 2)]
        flux_z = f * F[8, pl.ds(x, 2)]
        return f, 0.5 * (
            read(x + 1) * F[6, pl.ds(x + 1, 2)]
            - read(x - 1) * F[6, pl.ds(x - 1, 2)]
            + (up(flux_y, 1) - down(flux_y, 1))
            + (up(flux_z, 2) - down(flux_z, 2))
        )

    def adjoint_first(read):
        def body(x):
            f, rate = diverge(read, x)
            at_x = pl.ds(x, 2)
            T[0, at_x] = f + 0.5 * rate
            T[1, at_x] = f + 0.25 * rate

        return body

    def adjoint_second(x):
        f, rate = diverge(lambda i: T[0, pl.ds(i, 2)], x)
        at_x = pl.ds(x, 2)
        T[2, at_x] = T[1, at_x] + 0.25 * rate

    def adjoint_last(x):
        f, rate = diverge(lambda i: T[0, pl.ds(i, 2)], x)
        own = pl.ds(x, 2)
        at_x = pl.ds(x - W, 2)
        adj_zero = 0.125 * (T[1, own] + 0.25 * rate)[:, :ny]
        adj_one = 0.25 * T[2, own, pl.ds(0, ny)]
        for k in range(3):
            IMG[k, at_x] = IMG[k, at_x] + adj_one * G[3 + k, at_x] + adj_zero * G[k, at_x]

    sweep(1, ex - 2, 2, adjoint_first(lambda i: U[pl.ds(i, 2)]))
    sweep(2, ex - 4, 2, adjoint_second)
    sweep(3, ex - 6, 2, adjoint_first(lambda i: T[2, pl.ds(i, 2)]))
    sweep(4, ex - 8, 2, adjoint_last)

    for c in range(3):
        for b in range(cx):
            TR[3 + c, b] = jnp.sum(IMG[c, pl.ds(4 * b, 4)], axis=0)
    z_sums = jnp.dot(TR[...].reshape(n_rows, nz), gather_z, precision=HI, preferred_element_type=jnp.float32)
    rhs = jnp.dot(
        gather_y, jnp.where(keep, z_sums, 0.0), precision=HI, preferred_element_type=jnp.float32
    )
    CB[1, 1] = rhs.reshape(cx, 8, lanes)

    c_copies = []
    for i, (dx, dy) in enumerate(DIRS):
        c = mesh_copy(CB.at[1, 1], CB.at[1 - dx, 1 - dy], c_send.at[i], c_recv.at[i], dx, dy)
        c.start()
        c_copies.append(c)

    rq = jnp.zeros((ny, nz), jnp.float32)
    qq = jnp.zeros((ny, nz), jnp.float32)
    dq = jnp.zeros((ny, nz), jnp.float32)
    for c in range(3):
        for b in range(cx):
            q = IMG[c, pl.ds(4 * b, 4)]
            rq = rq + jnp.sum(q * RS[c, pl.ds(4 * b, 4)], axis=0)
            qq = qq + jnp.sum(q * q, axis=0)
            dq = dq + jnp.sum(q * F[3 + c, pl.ds(W + 4 * b, 4)][:, :ny], axis=0)
    flat = lambda v: jnp.sum(v, axis=0, keepdims=True)
    rr, rq, qq, dq = flat(rr), flat(rq), flat(qq), flat(dq)

    for c in c_copies:
        c.wait()
    b_all = jnp.concatenate(
        [jnp.concatenate([CB[a, e] for e in range(3)], axis=2) for a in range(3)], axis=0
    )
    b_all = b_all[cx - 3 : 2 * cx + 3]
    z_pos = lax.rem(lax.broadcasted_iota(jnp.int32, (1, 8, 3 * lanes), 2), cz)
    total_lanes = 3 * lanes
    approx = WEIGHT * b_all
    for turn in range(3):
        mid = approx[1:-1]
        z_up = jnp.where(z_pos == cz - 1, pltpu.roll(mid, cz - 1, 2), pltpu.roll(mid, total_lanes - 1, 2))
        z_down = jnp.where(z_pos == 0, pltpu.roll(mid, total_lanes - cz + 1, 2), pltpu.roll(mid, 1, 2))
        around = (
            approx[2:] + approx[:-2]
            + pltpu.roll(mid, cz, 2) + pltpu.roll(mid, total_lanes - cz, 2)
            + z_up + z_down
        )
        approx = 0.2 * mid + WEIGHT * (b_all[turn + 1 : -turn - 1] + 0.1 * around)
    e = approx[:, :, lanes : 2 * lanes]
    b_own = CB[1, 1]
    same = jnp.sum(b_own * e, axis=0)
    r8 = row((8, lanes))
    cross = jnp.sum(b_own * jnp.where(r8[None] < 3, pltpu.roll(e, 5, 1), pltpu.roll(e, 3, 1)), axis=0)
    pick = lambda v, lo, hi: flat(jnp.where(jnp.logical_and(r8 >= lo, r8 < hi), v, 0.0))
    sum_a = 0.25 * rr + 64.0 * pick(same, 0, 3)
    sum_b = 0.5 * rq + 64.0 * pick(cross, 0, 6)
    sum_c = 0.25 * qq + 64.0 * pick(same, 3, 6)
    whole = lambda v: jnp.broadcast_to(jnp.sum(v, axis=1, keepdims=True), (1, lanes))
    l1 = lane((1, lanes))
    AR[0] = jnp.where(
        l1 == 0, whole(sum_a), jnp.where(l1 == 1, whole(sum_b), jnp.where(l1 == 2, whole(sum_c), whole(dq)))
    )

    def sums_copy(d):
        other = peer(d)
        return pltpu.make_async_remote_copy(
            src_ref=AR.at[0], dst_ref=AR.at[d], send_sem=a_send.at[d], recv_sem=a_recv.at[d],
            device_id=other, device_id_type=pl.DeviceIdType.MESH,
        )

    each_peer(lambda d: sums_copy(d).start())

    spread = jnp.dot(spread_y, e.reshape(cx * 8, lanes), precision=HI, preferred_element_type=jnp.float32)
    fine = jnp.dot(jnp.where(keep, spread, 0.0), spread_z, precision=HI, preferred_element_type=jnp.float32)
    PR[...] = fine.reshape(6, cx, ny, nz)

    each_peer(lambda d: sums_copy(d).wait())
    sums = jnp.sum(AR[...], axis=0)
    rz, mixed, square, curvature = (
        jnp.sum(jnp.where(l1 == i, sums, 0.0), axis=1, keepdims=True) for i in range(4)
    )
    alpha = rz / curvature
    beta = (rz - alpha * mixed + alpha * alpha * square) / rz
    o_sc[...] = jnp.where(r8 == 0, alpha, beta)
    for c in locals_[4:]:
        c.wait()


def finish(scalars, coarse, image, keep, o_sol, o_res, o_dir, N, sem):
    alpha, beta = scalars[0:1, 0:1].reshape(1, 1, 1), scalars[1:2, 0:1].reshape(1, 1, 1)
    copies = []
    for c in range(3):
        for b in range(coarse.shape[1]):
            at_x = pl.ds(4 * b, 4)
            d = keep[1, c, at_x]
            left = keep[0, c, at_x] - alpha * image[c, at_x]
            mixed = coarse[c, pl.ds(b, 1)] - alpha * coarse[3 + c, pl.ds(b, 1)]
            N[0, c, at_x] = keep[2, c, at_x] + alpha * d
            N[1, c, at_x] = left
            N[2, c, at_x] = 0.25 * left + mixed + beta * d
        for i, out in enumerate((o_sol, o_res, o_dir)):
            copy = pltpu.make_async_copy(N.at[i, c], out.at[c], sem.at[3 * i + c])
            copy.start()
            copies.append(copy)
    for copy in copies:
        copy.wait()


def solution(mesh):
    px, py = mesh.shape["px"], mesh.shape["py"]
    spec = P(None, "px", "py", None)

    def local(velocity, states, solution, residual, direction):
        comps, nx, ny, nz = velocity.shape
        ex, ey = nx + 2 * W, ny + 2 * W
        cx = nx // 4
        lanes = (ny // 4) * (nz // 4)
        f32 = jnp.float32
        dma = pltpu.SemaphoreType.DMA
        shape = jax.ShapeDtypeStruct
        anywhere = pl.BlockSpec(memory_space=pl.ANY)
        vmem = pl.BlockSpec(memory_space=pltpu.VMEM)
        image, spread, scalars, keep = pl.pallas_call(
                functools.partial(kernel, px, py),
                out_shape=[
                    shape(velocity.shape, f32), shape((6, cx, ny, nz), f32), shape((8, lanes), f32),
                    shape((3,) + velocity.shape, f32),
                ],
                in_specs=[anywhere] * 5,
                out_specs=[vmem] * 4,
                scratch_shapes=[
                    pltpu.VMEM((9, ex, ey, nz), f32),
                    pltpu.VMEM((3, nx, 2 * W, nz), f32),
                    pltpu.VMEM((3, ex, ey, nz), f32),
                    pltpu.VMEM((4, ex, ey, nz), f32),
                    pltpu.VMEM((ex, ey, nz), f32),
                    pltpu.VMEM((9, nx, ny, nz), f32),
                    pltpu.VMEM((6, cx, ny, nz), f32),
                    pltpu.VMEM((3, 3, cx, 8, lanes), f32),
                    pltpu.VMEM((px * py, 1, lanes), f32),
                    dma((6,)),
                    dma((4, 8)),
                    dma((4, 8)),
                    dma((8,)),
                    dma((8,)),
                    dma((8,)),
                    dma((8,)),
                    dma((8,)),
                    dma((8,)),
                    dma((px * py,)),
                    dma((px * py,)),
                ],
                compiler_params=pltpu.CompilerParams(
                    collective_id=0, has_side_effects=True, vmem_limit_bytes=24 * 2**20
                ),
            )(*(pltpu.with_memory_space_constraint(a, pltpu.HBM) for a in (velocity, states, solution, residual, direction)))
        return tuple(
            pl.pallas_call(
                finish,
                out_shape=[shape(velocity.shape, f32)] * 3,
                in_specs=[vmem] * 4,
                out_specs=[anywhere] * 3,
                scratch_shapes=[pltpu.VMEM((3,) + velocity.shape, f32), dma((9,))],
                compiler_params=pltpu.CompilerParams(vmem_limit_bytes=8 * 2**20),
            )(scalars, spread, image, keep)
        )

    return jax.shard_map(local, mesh=mesh, in_specs=(spec,) * 5, out_specs=(spec,) * 3, check_vma=False)
```

```python
import functools

import jax
import jax.numpy as jnp
from jax import lax
from jax.experimental import pallas as pl
from jax.experimental.pallas import tpu as pltpu
from jax.sharding import PartitionSpec as P

W = 4
SIDES = ((0, 1), (0, -1), (1, 0), (-1, 0))
CORNERS = ((1, 1), (1, -1), (-1, 1), (-1, -1))
DIRS = SIDES + CORNERS
HI = lax.Precision.HIGHEST
WEIGHT = 0.8 / 0.65


def up(v, axis):
    return pltpu.roll(v, v.shape[axis] - 1, axis)


def down(v, axis):
    return pltpu.roll(v, 1, axis)


def kernel(
    px, py, vel, sta, sol, res, dirn, IMG, PR, o_sc, KEEP,
    F, FV, FC, S, T, U, G, CB, AR,
    loc_sem, h_send, h_recv, s_send, s_recv, u_send, u_recv, c_send, c_recv, a_send, a_recv,
):
    nx, ny, nz = sta.shape[1:]
    ex, ey = nx + 2 * W, ny + 2 * W
    me_x, me_y = lax.axis_index("px"), lax.axis_index("py")

    def at(dx, dy):
        return (lax.rem(me_x + (dx + px), px), lax.rem(me_y + (dy + py), py))

    def mesh_copy(src, dst, s, r, dx, dy):
        return pltpu.make_async_remote_copy(
            src_ref=src, dst_ref=dst, send_sem=s, recv_sem=r,
            device_id=at(dx, dy), device_id_type=pl.DeviceIdType.MESH,
        )

    locals_ = []
    for g, a in enumerate((sta, dirn, vel)):
        locals_.append(
            pltpu.make_async_copy(a, F.at[pl.ds(3 * g, 3), pl.ds(W, nx), pl.ds(0, ny)], loc_sem.at[g])
        )
    for i, a in enumerate((res, dirn, sol)):
        locals_.append(pltpu.make_async_copy(a, KEEP.at[i], loc_sem.at[3 + i]))
    RS = KEEP.at[0]

    barrier = pltpu.get_barrier_semaphore()
    total = px * py

    def peer(d):
        other = lax.rem(me_x * py + me_y + d, total)
        return (other // py, lax.rem(other, py))

    def each_peer(body):
        def run(i, carry):
            body(i + 1)
            return carry

        lax.fori_loop(0, total - 1, run, 0, unroll=total <= 64)

    small = max(px // 2 - 3, 0) + max(py // 2 - 3, 0) <= 2
    if small:
        for dx, dy in SIDES:
            pl.semaphore_signal(barrier, inc=1, device_id=at(dx, dy), device_id_type=pl.DeviceIdType.MESH)
    else:
        each_peer(
            lambda d: pl.semaphore_signal(
                barrier, inc=1, device_id=peer(d), device_id_type=pl.DeviceIdType.MESH
            )
        )
    for c in locals_:
        c.start()
    pl.semaphore_wait(barrier, len(SIDES) if small else total - 1)

    def x_span(dx, w, k):
        return {
            0: (0, nx, W),
            1: (nx - w - k, w, W - w - k),
            -1: (k, w, W + nx + k),
        }[dx]

    def y_span(dy, w, k):
        return {
            0: (0, ny, 0),
            1: (ny - w - k, w, ny + 2 * W - w - k),
            -1: (k, w, ny + k),
        }[dy]

    def halo(make, send, recv, dirs, width, base=0):
        copies = []
        for i, (dx, dy) in enumerate(dirs):
            sx, lx, tx = x_span(dx, width, base)
            sy, ly, ty = y_span(dy, width, base)
            src, dst = make((pl.ds(sx, lx), pl.ds(sy, ly)), (pl.ds(tx, lx), pl.ds(ty, ly)))
            copies.append(mesh_copy(src, dst, send.at[i], recv.at[i], dx, dy))
        for c in copies:
            c.start()
        return copies

    def field_halo(g, a, slot, *args):
        return halo(
            lambda src, dst: (a.at[(pl.ds(0, 3),) + src], F.at[(pl.ds(3 * g, 3),) + dst]),
            h_send.at[slot], h_recv.at[slot], *args,
        )

    state_copies = field_halo(0, sta, 0, SIDES, 1)
    near_copies = field_halo(2, vel, 1, SIDES, 2)

    row = lambda shape: lax.broadcasted_iota(jnp.int32, shape, 0)
    lane = lambda shape: lax.broadcasted_iota(jnp.int32, shape, 1)
    cz = nz // 4
    cx, cy = nx // 4, ny // 4
    lanes = cy * cz
    n_rows = 6 * cx * ny
    m_shape = (nz, lanes)
    gather_z = (row(m_shape) // 4 == lax.rem(lane(m_shape), cz)).astype(jnp.float32).astype(jnp.bfloat16)
    t_shape = (lanes, nz)
    spread_z = (lax.rem(row(t_shape), cz) == lane(t_shape) // 4).astype(jnp.float32)
    k_shape = (n_rows, lanes)
    keep = lax.rem(row(k_shape), ny) // 4 == lane(k_shape) // cz
    own_y = row((ny, lanes)) // 4 == lane((ny, lanes)) // cz
    p_shape = (n_rows, cx * 8)
    dst_c, dst_x = row(p_shape) // (cx * ny), lax.rem(row(p_shape) // ny, cx)
    spread_y = jnp.where(
        jnp.logical_and(lane(p_shape) // 8 == dst_x, lax.rem(lane(p_shape), 8) == dst_c), 1.0, 0.0
    )

    def sweep(start, planes, step, body):
        def run(i, carry):
            body(start + i * step)
            return carry

        lax.fori_loop(0, planes // step, run, 0, unroll=True)

    def restrict(read, first):
        x_sums = jnp.concatenate(
            [jnp.sum(read(c, pl.ds(4 * b, 4)), axis=0) for c in range(3) for b in range(cx)], axis=0
        )
        high = x_sums.astype(jnp.bfloat16)
        low = (x_sums - high.astype(jnp.float32)).astype(jnp.bfloat16)
        z_sums = jnp.dot(high, gather_z, preferred_element_type=jnp.float32) + jnp.dot(
            low, gather_z, preferred_element_type=jnp.float32
        )
        for c in range(3):
            for b in range(cx):
                at = (c * cx + b) * ny
                block = jnp.where(own_y, z_sums[at : at + ny], 0.0)
                CB[1, 1, b, pl.ds(first + c, 1)] = jnp.sum(block, axis=0, keepdims=True) * (1.0 / 64.0)

    def coarse_halo(first, slot):
        copies = []
        for i, (dx, dy) in enumerate(DIRS):
            xs = {0: pl.ds(0, cx), 1: pl.ds(cx - 3, 3), -1: pl.ds(0, 3)}[dx]
            rows = pl.ds(first, 3)
            copies.append(
                mesh_copy(
                    CB.at[1, 1, xs, rows], CB.at[1 - dx, 1 - dy, xs, rows],
                    c_send.at[slot, i], c_recv.at[slot, i], dx, dy,
                )
            )
        for c in copies:
            c.start()
        return copies

    locals_[3].wait()
    rr = jnp.zeros((ny, nz), jnp.float32)
    for c in range(3):
        for b in range(cx):
            r = RS[c, pl.ds(4 * b, 4)]
            rr = rr + jnp.sum(r * r, axis=0)
    restrict(lambda c, at: RS[c, at], 0)

    for c in locals_[:2]:
        c.wait()
    for c in state_copies:
        c.wait()

    def sources(x):
        own = pl.ds(x, 2)
        at_x = pl.ds(x - W, 2)
        d = [F[3 + k, own, pl.ds(0, ny)] for k in range(3)]
        for n in range(3):
            f = F[n, own]
            grads = (
                (F[n, pl.ds(x + 1, 2)] - F[n, pl.ds(x - 1, 2)])[:, :ny],
                (up(f, 1) - down(f, 1))[:, :ny],
                (up(f, 2) - down(f, 2))[:, :ny],
            )
            S[n, own, pl.ds(0, ny)] = 0.5 * (d[0] * grads[0] + d[1] * grads[1] + d[2] * grads[2])
            for k in range(3):
                G[3 * n + k, at_x] = grads[k]

    sweep(W, nx, 2, sources)
    def source_halo(lo, n, slot, dirs, width):
        return halo(
            lambda src, dst: (
                S.at[pl.ds(lo, n), pl.ds(W + src[0].start, src[0].size), src[1]],
                S.at[(pl.ds(lo, n),) + dst],
            ),
            s_send.at[slot], s_recv.at[slot], dirs, width,
        )

    source_copies = (
        source_halo(0, 2, 0, CORNERS, 2)
        + field_halo(2, vel, 4, CORNERS, 1)
        + source_halo(0, 1, 1, SIDES, 3)
        + source_halo(1, 1, 2, SIDES, 2)
    )
    far_copies = halo(
        lambda src, dst: (
            vel.at[(pl.ds(0, 3),) + src],
            FV.at[pl.ds(0, 3), pl.ds(0, nx), pl.ds(dst[1].start - ny, 2)]
            if dst[1].size == 2
            else F.at[(pl.ds(6, 3),) + dst],
        ),
        h_send.at[2], h_recv.at[2], SIDES, 2, 2,
    )
    far_copies += halo(
        lambda src, dst: (
            vel.at[(pl.ds(0, 3),) + src],
            FC.at[pl.ds(0, 3), int(dst[0].start > W), pl.ds(0, 3), pl.ds(dst[1].start - ny, 3)],
        ),
        h_send.at[5], h_recv.at[5], CORNERS, 3,
    )
    direction_copies = field_halo(1, dirn, 3, SIDES, 1)
    residual_coarse_copies = coarse_halo(0, 0)

    locals_[2].wait()
    for c in near_copies:
        c.wait()
    for c in source_copies:
        c.wait()

    def advect(read, x):
        f = read(x)
        v = [F[6 + k, pl.ds(x, 2)] for k in range(3)]
        return f, 0.5 * (
            v[0] * (read(x + 1) - read(x - 1))
            + v[1] * (up(f, 1) - down(f, 1))
            + v[2] * (up(f, 2) - down(f, 2))
        )

    def forward_one(x):
        f, adv = advect(lambda i: S[0, pl.ds(i, 2)], x)
        at_x = pl.ds(x, 2)
        T[1, at_x] = 0.25 * (0.5 * adv - S[1, at_x] - f)

    def forward_two(x):
        f, adv = advect(lambda i: T[1, pl.ds(i, 2)], x)
        at_x = pl.ds(x, 2)
        first = -(adv + S[1, at_x])
        T[2, at_x] = f + 0.5 * first
        T[3, at_x] = f + 0.25 * first

    def forward_three(x):
        f, adv = advect(lambda i: T[2, pl.ds(i, 2)], x)
        at_x = pl.ds(x, 2)
        U[at_x, pl.ds(0, ny)] = 0.25 * (adv[:, :ny] + S[2, at_x, pl.ds(0, ny)]) - T[3, at_x, pl.ds(0, ny)]

    sweep(2, ex - 4, 2, forward_one)
    sweep(3, ex - 6, 2, forward_two)
    sweep(4, ex - 8, 2, forward_three)

    def u_halo(slot, dirs, width):
        return halo(
            lambda src, dst: (U.at[pl.ds(W + src[0].start, src[0].size), src[1]], U.at[dst]),
            u_send.at[slot], u_recv.at[slot], dirs, width,
        )

    u_copies = u_halo(0, CORNERS, 3) + u_halo(1, SIDES, W)
    for c in direction_copies:
        c.wait()

    def base(x):
        own = pl.ds(x, 2)
        at_x = pl.ds(x - W, 2)
        adj = 0.125 * U[own, pl.ds(0, ny)]
        for k in range(3):
            f = F[3 + k, own]
            neighbours = (
                F[3 + k, pl.ds(x + 1, 2)] + F[3 + k, pl.ds(x - 1, 2)]
                + up(f, 1) + down(f, 1) + up(f, 2) + down(f, 2)
            )[:, :ny]
            IMG[k, at_x] = 4.0 * f[:, :ny] - 0.5 * neighbours + adj * G[6 + k, at_x]

    sweep(W, nx, 2, base)
    for c in far_copies:
        c.wait()
    tile_row = lax.broadcasted_iota(jnp.int32, (1, 1, 2 * W, nz), 2)
    band, beyond = pl.ds(W, nx), pl.ds(ny, 2 * W)
    from_far = jnp.logical_and(tile_row >= 2, tile_row < 2 * W - 2)
    F[pl.ds(6, 3), band, beyond] = jnp.where(from_far, FV[...], F[pl.ds(6, 3), band, beyond])
    F[pl.ds(6, 3), pl.ds(W - 3, 3), beyond] = FC[:, 0]
    F[pl.ds(6, 3), pl.ds(W + nx, 3), beyond] = FC[:, 1]
    for c in u_copies:
        c.wait()

    def diverge(read, x):
        f = read(x)
        flux_y = f * F[7, pl.ds(x, 2)]
        flux_z = f * F[8, pl.ds(x, 2)]
        return f, 0.5 * (
            read(x + 1) * F[6, pl.ds(x + 1, 2)]
            - read(x - 1) * F[6, pl.ds(x - 1, 2)]
            + (up(flux_y, 1) - down(flux_y, 1))
            + (up(flux_z, 2) - down(flux_z, 2))
        )

    def adjoint_first(read):
        def body(x):
            f, rate = diverge(read, x)
            at_x = pl.ds(x, 2)
            T[0, at_x] = f + 0.5 * rate
            T[1, at_x] = f + 0.25 * rate

        return body

    def adjoint_second(x):
        f, rate = diverge(lambda i: T[0, pl.ds(i, 2)], x)
        at_x = pl.ds(x, 2)
        T[2, at_x] = T[1, at_x] + 0.25 * rate

    def adjoint_last(x):
        f, rate = diverge(lambda i: T[0, pl.ds(i, 2)], x)
        own = pl.ds(x, 2)
        at_x = pl.ds(x - W, 2)
        adj_zero = 0.125 * (T[1, own] + 0.25 * rate)[:, :ny]
        adj_one = 0.25 * T[2, own, pl.ds(0, ny)]
        for k in range(3):
            IMG[k, at_x] = IMG[k, at_x] + adj_one * G[3 + k, at_x] + adj_zero * G[k, at_x]

    sweep(1, ex - 2, 2, adjoint_first(lambda i: U[pl.ds(i, 2)]))
    sweep(2, ex - 4, 2, adjoint_second)
    sweep(3, ex - 6, 2, adjoint_first(lambda i: T[2, pl.ds(i, 2)]))
    sweep(4, ex - 8, 2, adjoint_last)

    restrict(lambda c, at: IMG[c, at], 3)
    c_copies = residual_coarse_copies + coarse_halo(3, 1)

    rq = jnp.zeros((ny, nz), jnp.float32)
    qq = jnp.zeros((ny, nz), jnp.float32)
    dq = jnp.zeros((ny, nz), jnp.float32)
    for c in range(3):
        for b in range(cx):
            q = IMG[c, pl.ds(4 * b, 4)]
            rq = rq + jnp.sum(q * RS[c, pl.ds(4 * b, 4)], axis=0)
            qq = qq + jnp.sum(q * q, axis=0)
            dq = dq + jnp.sum(q * F[3 + c, pl.ds(W + 4 * b, 4)][:, :ny], axis=0)
    flat = lambda v: jnp.sum(v, axis=0, keepdims=True)
    rr, rq, qq, dq = flat(rr), flat(rq), flat(qq), flat(dq)

    for c in c_copies:
        c.wait()
    b_all = jnp.concatenate(
        [jnp.concatenate([CB[a, e] for e in range(3)], axis=2) for a in range(3)], axis=0
    )
    b_all = b_all[cx - 3 : 2 * cx + 3]
    z_pos = lax.rem(lax.broadcasted_iota(jnp.int32, (1, 8, 3 * lanes), 2), cz)
    total_lanes = 3 * lanes
    approx = WEIGHT * b_all
    for turn in range(3):
        mid = approx[1:-1]
        z_up = jnp.where(z_pos == cz - 1, pltpu.roll(mid, cz - 1, 2), pltpu.roll(mid, total_lanes - 1, 2))
        z_down = jnp.where(z_pos == 0, pltpu.roll(mid, total_lanes - cz + 1, 2), pltpu.roll(mid, 1, 2))
        around = (
            approx[2:] + approx[:-2]
            + pltpu.roll(mid, cz, 2) + pltpu.roll(mid, total_lanes - cz, 2)
            + z_up + z_down
        )
        approx = 0.2 * mid + WEIGHT * (b_all[turn + 1 : -turn - 1] + 0.1 * around)
    r8 = row((8, lanes))
    e = jnp.where(r8[None] < 6, approx[:, :, lanes : 2 * lanes], 0.0)
    b_own = CB[1, 1]
    same = jnp.sum(b_own * e, axis=0)
    cross = jnp.sum(b_own * jnp.where(r8[None] < 3, pltpu.roll(e, 5, 1), pltpu.roll(e, 3, 1)), axis=0)
    pick = lambda v, lo, hi: flat(jnp.where(jnp.logical_and(r8 >= lo, r8 < hi), v, 0.0))
    sum_a = 0.25 * rr + 64.0 * pick(same, 0, 3)
    sum_b = 0.5 * rq + 64.0 * pick(cross, 0, 6)
    sum_c = 0.25 * qq + 64.0 * pick(same, 3, 6)
    whole = lambda v: jnp.broadcast_to(jnp.sum(v, axis=1, keepdims=True), (1, lanes))
    l1 = lane((1, lanes))
    AR[0] = jnp.where(
        l1 == 0, whole(sum_a), jnp.where(l1 == 1, whole(sum_b), jnp.where(l1 == 2, whole(sum_c), whole(dq)))
    )

    def sums_copy(d):
        other = peer(d)
        return pltpu.make_async_remote_copy(
            src_ref=AR.at[0], dst_ref=AR.at[d], send_sem=a_send.at[d], recv_sem=a_recv.at[d],
            device_id=other, device_id_type=pl.DeviceIdType.MESH,
        )

    each_peer(lambda d: sums_copy(d).start())

    spread = jnp.dot(spread_y, e.reshape(cx * 8, lanes), precision=HI, preferred_element_type=jnp.float32)
    fine = jnp.dot(jnp.where(keep, spread, 0.0), spread_z, precision=HI, preferred_element_type=jnp.float32)
    PR[...] = fine.reshape(6, cx, ny, nz)

    each_peer(lambda d: sums_copy(d).wait())
    sums = jnp.sum(AR[...], axis=0)
    rz, mixed, square, curvature = (
        jnp.sum(jnp.where(l1 == i, sums, 0.0), axis=1, keepdims=True) for i in range(4)
    )
    alpha = rz / curvature
    beta = (rz - alpha * mixed + alpha * alpha * square) / rz
    o_sc[...] = jnp.where(r8 == 0, alpha, beta)
    for c in locals_[4:]:
        c.wait()


def finish(scalars, coarse, image, keep, o_sol, o_res, o_dir, N, sem):
    alpha, beta = scalars[0:1, 0:1].reshape(1, 1, 1), scalars[1:2, 0:1].reshape(1, 1, 1)
    copies = []
    for c in range(3):
        for b in range(coarse.shape[1]):
            at_x = pl.ds(4 * b, 4)
            d = keep[1, c, at_x]
            left = keep[0, c, at_x] - alpha * image[c, at_x]
            mixed = coarse[c, pl.ds(b, 1)] - alpha * coarse[3 + c, pl.ds(b, 1)]
            N[0, c, at_x] = keep[2, c, at_x] + alpha * d
            N[1, c, at_x] = left
            N[2, c, at_x] = 0.25 * left + mixed + beta * d
        for i, out in enumerate((o_sol, o_res, o_dir)):
            copy = pltpu.make_async_copy(N.at[i, c], out.at[c], sem.at[3 * i + c])
            copy.start()
            copies.append(copy)
    for copy in copies:
        copy.wait()


def solution(mesh):
    px, py = mesh.shape["px"], mesh.shape["py"]
    spec = P(None, "px", "py", None)

    def local(velocity, states, solution, residual, direction):
        comps, nx, ny, nz = velocity.shape
        ex, ey = nx + 2 * W, ny + 2 * W
        cx = nx // 4
        lanes = (ny // 4) * (nz // 4)
        f32 = jnp.float32
        dma = pltpu.SemaphoreType.DMA
        shape = jax.ShapeDtypeStruct
        anywhere = pl.BlockSpec(memory_space=pl.ANY)
        vmem = pl.BlockSpec(memory_space=pltpu.VMEM)
        image, spread, scalars, keep = pl.pallas_call(
                functools.partial(kernel, px, py),
                out_shape=[
                    shape(velocity.shape, f32), shape((6, cx, ny, nz), f32), shape((8, lanes), f32),
                    shape((3,) + velocity.shape, f32),
                ],
                in_specs=[anywhere] * 5,
                out_specs=[vmem] * 4,
                scratch_shapes=[
                    pltpu.VMEM((9, ex, ey, nz), f32),
                    pltpu.VMEM((3, nx, 2 * W, nz), f32),
                    pltpu.VMEM((3, 2, 3, 2 * W, nz), f32),
                    pltpu.VMEM((3, ex, ey, nz), f32),
                    pltpu.VMEM((4, ex, ey, nz), f32),
                    pltpu.VMEM((ex, ey, nz), f32),
                    pltpu.VMEM((9, nx, ny, nz), f32),
                    pltpu.VMEM((3, 3, cx, 8, lanes), f32),
                    pltpu.VMEM((px * py, 1, lanes), f32),
                    dma((6,)),
                    dma((6, 4)),
                    dma((6, 4)),
                    dma((3, 4)),
                    dma((3, 4)),
                    dma((2, 4)),
                    dma((2, 4)),
                    dma((2, 8)),
                    dma((2, 8)),
                    dma((px * py,)),
                    dma((px * py,)),
                ],
                compiler_params=pltpu.CompilerParams(
                    collective_id=0, has_side_effects=True, vmem_limit_bytes=24 * 2**20
                ),
            )(*(pltpu.with_memory_space_constraint(a, pltpu.HBM) for a in (velocity, states, solution, residual, direction)))
        return tuple(
            pl.pallas_call(
                finish,
                out_shape=[shape(velocity.shape, f32)] * 3,
                in_specs=[vmem] * 4,
                out_specs=[anywhere] * 3,
                scratch_shapes=[pltpu.VMEM((3,) + velocity.shape, f32), dma((9,))],
                compiler_params=pltpu.CompilerParams(vmem_limit_bytes=8 * 2**20),
            )(scalars, spread, image, keep)
        )

    return jax.shard_map(local, mesh=mesh, in_specs=(spec,) * 5, out_specs=(spec,) * 3, check_vma=False)
```

```python
import functools

import jax
import jax.numpy as jnp
from jax import lax
from jax.experimental import pallas as pl
from jax.experimental.pallas import tpu as pltpu
from jax.sharding import PartitionSpec as P

W = 4
SIDES = ((0, 1), (0, -1), (1, 0), (-1, 0))
CORNERS = ((1, 1), (1, -1), (-1, 1), (-1, -1))
DIRS = SIDES + CORNERS
HI = lax.Precision.HIGHEST
WEIGHT = 0.8 / 0.65


def up(v, axis):
    return pltpu.roll(v, v.shape[axis] - 1, axis)


def down(v, axis):
    return pltpu.roll(v, 1, axis)


def kernel(
    px, py, vel, sta, sol, res, dirn, IMG, PR, o_sc, KEEP,
    F, FV, FC, S, T, U, G, CB, AR,
    loc_sem, h_send, h_recv, s_send, s_recv, u_send, u_recv, c_send, c_recv, a_send, a_recv,
):
    nx, ny, nz = sta.shape[1:]
    ex, ey = nx + 2 * W, ny + 2 * W
    me_x, me_y = lax.axis_index("px"), lax.axis_index("py")

    def at(dx, dy):
        return (lax.rem(me_x + (dx + px), px), lax.rem(me_y + (dy + py), py))

    def mesh_copy(src, dst, s, r, dx, dy):
        return pltpu.make_async_remote_copy(
            src_ref=src, dst_ref=dst, send_sem=s, recv_sem=r,
            device_id=at(dx, dy), device_id_type=pl.DeviceIdType.MESH,
        )

    locals_ = []
    for g, a in enumerate((sta, dirn, vel)):
        locals_.append(
            pltpu.make_async_copy(a, F.at[pl.ds(3 * g, 3), pl.ds(W, nx), pl.ds(0, ny)], loc_sem.at[g])
        )
    for i, a in enumerate((res, dirn, sol)):
        locals_.append(pltpu.make_async_copy(a, KEEP.at[i], loc_sem.at[3 + i]))
    RS = KEEP.at[0]

    barrier = pltpu.get_barrier_semaphore()
    total = px * py

    def peer(d):
        other = lax.rem(me_x * py + me_y + d, total)
        return (other // py, lax.rem(other, py))

    def each_peer(body):
        def run(i, carry):
            body(i + 1)
            return carry

        lax.fori_loop(0, total - 1, run, 0, unroll=total <= 64)

    small = max(px // 2 - 3, 0) + max(py // 2 - 3, 0) <= 2
    if small:
        for dx, dy in SIDES:
            pl.semaphore_signal(barrier, inc=1, device_id=at(dx, dy), device_id_type=pl.DeviceIdType.MESH)
    else:
        each_peer(
            lambda d: pl.semaphore_signal(
                barrier, inc=1, device_id=peer(d), device_id_type=pl.DeviceIdType.MESH
            )
        )
    for c in locals_:
        c.start()
    pl.semaphore_wait(barrier, len(SIDES) if small else total - 1)

    def x_span(dx, w, k):
        return {
            0: (0, nx, W),
            1: (nx - w - k, w, W - w - k),
            -1: (k, w, W + nx + k),
        }[dx]

    def y_span(dy, w, k):
        return {
            0: (0, ny, 0),
            1: (ny - w - k, w, ny + 2 * W - w - k),
            -1: (k, w, ny + k),
        }[dy]

    def halo(make, send, recv, dirs, width, base=0):
        copies = []
        for i, (dx, dy) in enumerate(dirs):
            sx, lx, tx = x_span(dx, width, base)
            sy, ly, ty = y_span(dy, width, base)
            src, dst = make((pl.ds(sx, lx), pl.ds(sy, ly)), (pl.ds(tx, lx), pl.ds(ty, ly)))
            copies.append(mesh_copy(src, dst, send.at[i], recv.at[i], dx, dy))
        return copies

    def launch(copies):
        for c in copies:
            c.start()
        return copies

    def own(g, src):
        return F.at[pl.ds(3 * g, 3), pl.ds(W + src[0].start, src[0].size), src[1]]

    def field_halo(g, slot, *args):
        return halo(
            lambda src, dst: (own(g, src), F.at[(pl.ds(3 * g, 3),) + dst]),
            h_send.at[slot], h_recv.at[slot], *args,
        )

    locals_[0].wait()
    state_copies = launch(field_halo(0, 0, SIDES, 1))
    locals_[2].wait()
    near_copies = launch(field_halo(2, 1, SIDES, 2))

    row = lambda shape: lax.broadcasted_iota(jnp.int32, shape, 0)
    lane = lambda shape: lax.broadcasted_iota(jnp.int32, shape, 1)
    cz = nz // 4
    cx, cy = nx // 4, ny // 4
    lanes = cy * cz
    m_shape = (nz, lanes)
    gather_z = (row(m_shape) // 4 == lax.rem(lane(m_shape), cz)).astype(jnp.float32).astype(jnp.bfloat16)
    t_shape = (lanes, nz)
    spread_z = (lax.rem(row(t_shape), cz) == lane(t_shape) // 4).astype(jnp.float32).astype(jnp.bfloat16)
    own_y = row((ny, lanes)) // 4 == lane((ny, lanes)) // cz
    def sweep(start, planes, step, body):
        def run(i, carry):
            body(start + i * step)
            return carry

        lax.fori_loop(0, planes // step, run, 0, unroll=True)

    def two_terms(v, exact):
        high = v.astype(jnp.bfloat16)
        low = (v - high.astype(jnp.float32)).astype(jnp.bfloat16)
        return sum(jnp.dot(part, exact, preferred_element_type=jnp.float32) for part in (low, high))

    def restrict(read, first):
        x_sums = jnp.concatenate(
            [jnp.sum(read(c, pl.ds(4 * b, 4)), axis=0) for c in range(3) for b in range(cx)], axis=0
        )
        z_sums = two_terms(x_sums, gather_z)
        for c in range(3):
            for b in range(cx):
                at = (c * cx + b) * ny
                block = jnp.where(own_y, z_sums[at : at + ny], 0.0)
                CB[1, 1, b, pl.ds(first + c, 1)] = jnp.sum(block, axis=0, keepdims=True) * (1.0 / 64.0)

    def coarse_halo(first, slot):
        copies = []
        for i, (dx, dy) in enumerate(CORNERS + SIDES):
            xs = {0: pl.ds(0, cx), 1: pl.ds(cx - 3, 3), -1: pl.ds(0, 3)}[dx]
            rows = pl.ds(first, 3)
            c = mesh_copy(
                CB.at[1, 1, xs, rows], CB.at[1 - dx, 1 - dy, xs, rows],
                c_send.at[slot, i], c_recv.at[slot, i], dx, dy,
            )
            copies.append(c)
        return launch(copies)

    locals_[3].wait()
    rr = jnp.zeros((ny, nz), jnp.float32)
    for c in range(3):
        for b in range(cx):
            r = RS[c, pl.ds(4 * b, 4)]
            rr = rr + jnp.sum(r * r, axis=0)
    restrict(lambda c, at: RS[c, at], 0)

    locals_[1].wait()
    for c in state_copies:
        c.wait()

    def gradient(n, x):
        f = F[n, pl.ds(x, 2)]
        return (
            (F[n, pl.ds(x + 1, 2)] - F[n, pl.ds(x - 1, 2)])[:, :ny],
            (up(f, 1) - down(f, 1))[:, :ny],
            (up(f, 2) - down(f, 2))[:, :ny],
        )

    def sources(moments):
        def body(x):
            own = pl.ds(x, 2)
            d = [F[3 + k, own, pl.ds(0, ny)] for k in range(3)]
            for n in moments:
                grads = gradient(n, x)
                S[n, own, pl.ds(0, ny)] = 0.5 * (d[0] * grads[0] + d[1] * grads[1] + d[2] * grads[2])
                for k in range(3):
                    G[3 * n + k, pl.ds(x - W, 2)] = grads[k]

        return body

    sweep(W, nx, 2, sources((0, 1)))
    def source_halo(lo, n, slot, dirs, width):
        return halo(
            lambda src, dst: (
                S.at[pl.ds(lo, n), pl.ds(W + src[0].start, src[0].size), src[1]],
                S.at[(pl.ds(lo, n),) + dst],
            ),
            s_send.at[slot], s_recv.at[slot], dirs, width,
        )

    source_copies = launch(
        source_halo(0, 2, 0, CORNERS, 2)
        + field_halo(2, 4, CORNERS, 1)
        + source_halo(0, 1, 1, SIDES, 3)
        + source_halo(1, 1, 2, SIDES, 2)
    )
    far_copies = halo(
        lambda src, dst: (
            own(2, src),
            FV.at[pl.ds(0, 3), pl.ds(0, nx), pl.ds(dst[1].start - ny, 2)]
            if dst[1].size == 2
            else F.at[(pl.ds(6, 3),) + dst],
        ),
        h_send.at[2], h_recv.at[2], SIDES, 2, 2,
    )
    far_copies += halo(
        lambda src, dst: (
            own(2, src),
            FC.at[pl.ds(0, 3), int(dst[0].start > W), pl.ds(0, 3), pl.ds(dst[1].start - ny, 3)],
        ),
        h_send.at[5], h_recv.at[5], CORNERS, 3,
    )
    far_copies = launch(far_copies)
    direction_copies = launch(field_halo(1, 3, SIDES, 1))
    residual_coarse_copies = coarse_halo(0, 0)
    sweep(W, nx, 2, sources((2,)))

    for c in near_copies:
        c.wait()
    for c in source_copies:
        c.wait()

    def advect(read, x):
        f = read(x)
        v = [F[6 + k, pl.ds(x, 2)] for k in range(3)]
        return f, 0.5 * (
            v[0] * (read(x + 1) - read(x - 1))
            + v[1] * (up(f, 1) - down(f, 1))
            + v[2] * (up(f, 2) - down(f, 2))
        )

    def forward_one(x):
        f, adv = advect(lambda i: S[0, pl.ds(i, 2)], x)
        at_x = pl.ds(x, 2)
        T[1, at_x] = 0.25 * (0.5 * adv - S[1, at_x] - f)

    def forward_two(x):
        f, adv = advect(lambda i: T[1, pl.ds(i, 2)], x)
        at_x = pl.ds(x, 2)
        first = -(adv + S[1, at_x])
        T[2, at_x] = f + 0.5 * first
        T[3, at_x] = f + 0.25 * first

    def forward_three(x):
        f, adv = advect(lambda i: T[2, pl.ds(i, 2)], x)
        at_x = pl.ds(x, 2)
        U[at_x, pl.ds(0, ny)] = 0.25 * (adv[:, :ny] + S[2, at_x, pl.ds(0, ny)]) - T[3, at_x, pl.ds(0, ny)]

    sweep(2, ex - 4, 2, forward_one)
    sweep(3, ex - 6, 2, forward_two)
    sweep(4, ex - 8, 2, forward_three)

    def u_halo(slot, dirs, width):
        return halo(
            lambda src, dst: (U.at[pl.ds(W + src[0].start, src[0].size), src[1]], U.at[dst]),
            u_send.at[slot], u_recv.at[slot], dirs, width,
        )

    u_copies = launch(u_halo(0, CORNERS, 3) + u_halo(1, SIDES, W))
    for c in direction_copies:
        c.wait()

    def base(x):
        own = pl.ds(x, 2)
        at_x = pl.ds(x - W, 2)
        adj = 0.125 * U[own, pl.ds(0, ny)]
        for k in range(3):
            f = F[3 + k, own]
            neighbours = (
                F[3 + k, pl.ds(x + 1, 2)] + F[3 + k, pl.ds(x - 1, 2)]
                + up(f, 1) + down(f, 1) + up(f, 2) + down(f, 2)
            )[:, :ny]
            IMG[k, at_x] = 4.0 * f[:, :ny] - 0.5 * neighbours + adj * G[6 + k, at_x]

    sweep(W, nx, 2, base)
    for c in far_copies:
        c.wait()
    tile_row = lax.broadcasted_iota(jnp.int32, (1, 1, 2 * W, nz), 2)
    band, beyond = pl.ds(W, nx), pl.ds(ny, 2 * W)
    from_far = jnp.logical_and(tile_row >= 2, tile_row < 2 * W - 2)
    F[pl.ds(6, 3), band, beyond] = jnp.where(from_far, FV[...], F[pl.ds(6, 3), band, beyond])
    F[pl.ds(6, 3), pl.ds(W - 3, 3), beyond] = FC[:, 0]
    F[pl.ds(6, 3), pl.ds(W + nx, 3), beyond] = FC[:, 1]
    for c in u_copies:
        c.wait()

    def diverge(read, x):
        f = read(x)
        flux_y = f * F[7, pl.ds(x, 2)]
        flux_z = f * F[8, pl.ds(x, 2)]
        return f, 0.5 * (
            read(x + 1) * F[6, pl.ds(x + 1, 2)]
            - read(x - 1) * F[6, pl.ds(x - 1, 2)]
            + (up(flux_y, 1) - down(flux_y, 1))
            + (up(flux_z, 2) - down(flux_z, 2))
        )

    def adjoint_first(read):
        def body(x):
            f, rate = diverge(read, x)
            at_x = pl.ds(x, 2)
            T[0, at_x] = f + 0.5 * rate
            T[1, at_x] = f + 0.25 * rate

        return body

    def adjoint_second(x):
        f, rate = diverge(lambda i: T[0, pl.ds(i, 2)], x)
        at_x = pl.ds(x, 2)
        T[2, at_x] = T[1, at_x] + 0.25 * rate

    def adjoint_last(x):
        f, rate = diverge(lambda i: T[0, pl.ds(i, 2)], x)
        own = pl.ds(x, 2)
        at_x = pl.ds(x - W, 2)
        adj_zero = 0.125 * (T[1, own] + 0.25 * rate)[:, :ny]
        adj_one = 0.25 * T[2, own, pl.ds(0, ny)]
        for k in range(3):
            IMG[k, at_x] = IMG[k, at_x] + adj_one * G[3 + k, at_x] + adj_zero * G[k, at_x]

    sweep(1, ex - 2, 2, adjoint_first(lambda i: U[pl.ds(i, 2)]))
    sweep(2, ex - 4, 2, adjoint_second)
    sweep(3, ex - 6, 2, adjoint_first(lambda i: T[2, pl.ds(i, 2)]))
    sweep(4, ex - 8, 2, adjoint_last)

    restrict(lambda c, at: IMG[c, at], 3)
    c_copies = residual_coarse_copies + coarse_halo(3, 1)

    rq = jnp.zeros((ny, nz), jnp.float32)
    qq = jnp.zeros((ny, nz), jnp.float32)
    dq = jnp.zeros((ny, nz), jnp.float32)
    for c in range(3):
        for b in range(cx):
            q = IMG[c, pl.ds(4 * b, 4)]
            rq = rq + jnp.sum(q * RS[c, pl.ds(4 * b, 4)], axis=0)
            qq = qq + jnp.sum(q * q, axis=0)
            dq = dq + jnp.sum(q * F[3 + c, pl.ds(W + 4 * b, 4)][:, :ny], axis=0)
    flat = lambda v: jnp.sum(v, axis=0, keepdims=True)
    rr, rq, qq, dq = flat(rr), flat(rq), flat(qq), flat(dq)

    for c in c_copies:
        c.wait()
    b_all = jnp.concatenate(
        [jnp.concatenate([CB[a, e] for e in range(3)], axis=2) for a in range(3)], axis=0
    )
    b_all = b_all[cx - 3 : 2 * cx + 3]
    z_pos = lax.rem(lax.broadcasted_iota(jnp.int32, (1, 8, 3 * lanes), 2), cz)
    total_lanes = 3 * lanes
    approx = WEIGHT * b_all
    for turn in range(3):
        mid = approx[1:-1]
        z_up = jnp.where(z_pos == cz - 1, pltpu.roll(mid, cz - 1, 2), pltpu.roll(mid, total_lanes - 1, 2))
        z_down = jnp.where(z_pos == 0, pltpu.roll(mid, total_lanes - cz + 1, 2), pltpu.roll(mid, 1, 2))
        around = (
            approx[2:] + approx[:-2]
            + pltpu.roll(mid, cz, 2) + pltpu.roll(mid, total_lanes - cz, 2)
            + z_up + z_down
        )
        approx = 0.2 * mid + WEIGHT * (b_all[turn + 1 : -turn - 1] + 0.1 * around)
    r8 = row((8, lanes))
    e = jnp.where(r8[None] < 6, approx[:, :, lanes : 2 * lanes], 0.0)
    b_own = CB[1, 1]
    same = jnp.sum(b_own * e, axis=0)
    cross = jnp.sum(b_own * jnp.where(r8[None] < 3, pltpu.roll(e, 5, 1), pltpu.roll(e, 3, 1)), axis=0)
    pick = lambda v, lo, hi: flat(jnp.where(jnp.logical_and(r8 >= lo, r8 < hi), v, 0.0))
    sum_a = 0.25 * rr + 64.0 * pick(same, 0, 3)
    sum_b = 0.5 * rq + 64.0 * pick(cross, 0, 6)
    sum_c = 0.25 * qq + 64.0 * pick(same, 3, 6)
    whole = lambda v: jnp.broadcast_to(jnp.sum(v, axis=1, keepdims=True), (1, lanes))
    l1 = lane((1, lanes))
    AR[0] = jnp.where(
        l1 == 0, whole(sum_a), jnp.where(l1 == 1, whole(sum_b), jnp.where(l1 == 2, whole(sum_c), whole(dq)))
    )

    around_x = [lax.rem(me_x + i, px) for i in range(px)]
    around_y = [lax.rem(me_y + j, py) for j in range(py)]

    def sums_copy(d):
        other = (around_x[d // py], around_y[d % py]) if isinstance(d, int) else peer(d)
        return pltpu.make_async_remote_copy(
            src_ref=AR.at[0], dst_ref=AR.at[d], send_sem=a_send.at[d], recv_sem=a_recv.at[d],
            device_id=other, device_id_type=pl.DeviceIdType.MESH,
        )

    if total <= 64:
        far_y = sorted(range(py), key=lambda j: -abs(2 * j - py) if j else 1)
        far_x = sorted(range(px), key=lambda i: abs(2 * i - px))
        order = [i * py + j for j in far_y for i in far_x if i or j]
        for d in order:
            sums_copy(d).start()
    else:
        each_peer(lambda d: sums_copy(d).start())

    wide = jnp.concatenate(
        [jnp.where(own_y, e[b, c : c + 1], 0.0) for c in range(6) for b in range(cx)], axis=0
    )
    PR[...] = two_terms(wide, spread_z).reshape(6, cx, ny, nz)

    if total <= 64:
        for d in range(1, total):
            sums_copy(d).wait()
    else:
        each_peer(lambda d: sums_copy(d).wait())
    sums = jnp.sum(AR[...], axis=0)
    rz, mixed, square, curvature = (
        jnp.sum(jnp.where(l1 == i, sums, 0.0), axis=1, keepdims=True) for i in range(4)
    )
    alpha = rz / curvature
    beta = (rz - alpha * mixed + alpha * alpha * square) / rz
    o_sc[...] = jnp.where(r8 == 0, alpha, beta)
    for c in locals_[4:]:
        c.wait()


def finish(scalars, coarse, image, keep, o_sol, o_res, o_dir, N, sem):
    alpha, beta = scalars[0:1, 0:1].reshape(1, 1, 1), scalars[1:2, 0:1].reshape(1, 1, 1)
    copies = []
    for c in range(3):
        for b in range(coarse.shape[1]):
            at_x = pl.ds(4 * b, 4)
            d = keep[1, c, at_x]
            left = keep[0, c, at_x] - alpha * image[c, at_x]
            mixed = coarse[c, pl.ds(b, 1)] - alpha * coarse[3 + c, pl.ds(b, 1)]
            N[0, c, at_x] = keep[2, c, at_x] + alpha * d
            N[1, c, at_x] = left
            N[2, c, at_x] = 0.25 * left + mixed + beta * d
        for i, out in enumerate((o_sol, o_res, o_dir)):
            copy = pltpu.make_async_copy(N.at[i, c], out.at[c], sem.at[3 * i + c])
            copy.start()
            copies.append(copy)
    for copy in copies:
        copy.wait()


def solution(mesh):
    px, py = mesh.shape["px"], mesh.shape["py"]
    spec = P(None, "px", "py", None)

    def local(velocity, states, solution, residual, direction):
        comps, nx, ny, nz = velocity.shape
        ex, ey = nx + 2 * W, ny + 2 * W
        cx = nx // 4
        lanes = (ny // 4) * (nz // 4)
        f32 = jnp.float32
        dma = pltpu.SemaphoreType.DMA
        shape = jax.ShapeDtypeStruct
        anywhere = pl.BlockSpec(memory_space=pl.ANY)
        vmem = pl.BlockSpec(memory_space=pltpu.VMEM)
        image, spread, scalars, keep = pl.pallas_call(
                functools.partial(kernel, px, py),
                out_shape=[
                    shape(velocity.shape, f32), shape((6, cx, ny, nz), f32), shape((8, lanes), f32),
                    shape((3,) + velocity.shape, f32),
                ],
                in_specs=[anywhere] * 5,
                out_specs=[vmem] * 4,
                scratch_shapes=[
                    pltpu.VMEM((9, ex, ey, nz), f32),
                    pltpu.VMEM((3, nx, 2 * W, nz), f32),
                    pltpu.VMEM((3, 2, 3, 2 * W, nz), f32),
                    pltpu.VMEM((3, ex, ey, nz), f32),
                    pltpu.VMEM((4, ex, ey, nz), f32),
                    pltpu.VMEM((ex, ey, nz), f32),
                    pltpu.VMEM((9, nx, ny, nz), f32),
                    pltpu.VMEM((3, 3, cx, 8, lanes), f32),
                    pltpu.VMEM((px * py, 1, lanes), f32),
                    dma((6,)),
                    dma((6, 4)),
                    dma((6, 4)),
                    dma((3, 4)),
                    dma((3, 4)),
                    dma((2, 4)),
                    dma((2, 4)),
                    dma((2, 8)),
                    dma((2, 8)),
                    dma((px * py,)),
                    dma((px * py,)),
                ],
                compiler_params=pltpu.CompilerParams(
                    collective_id=0, has_side_effects=True, vmem_limit_bytes=24 * 2**20
                ),
            )(*(pltpu.with_memory_space_constraint(a, pltpu.HBM) for a in (velocity, states, solution, residual, direction)))
        return tuple(
            pl.pallas_call(
                finish,
                out_shape=[shape(velocity.shape, f32)] * 3,
                in_specs=[vmem] * 4,
                out_specs=[anywhere] * 3,
                scratch_shapes=[pltpu.VMEM((3,) + velocity.shape, f32), dma((9,))],
                compiler_params=pltpu.CompilerParams(vmem_limit_bytes=8 * 2**20),
            )(scalars, spread, image, keep)
        )

    return jax.shard_map(local, mesh=mesh, in_specs=(spec,) * 5, out_specs=(spec,) * 3, check_vma=False)
```

```python
import functools

import jax
import jax.numpy as jnp
from jax import lax
from jax.experimental import pallas as pl
from jax.experimental.pallas import tpu as pltpu
from jax.sharding import PartitionSpec as P

W = 4
SIDES = ((0, 1), (0, -1), (1, 0), (-1, 0))
CORNERS = ((1, 1), (1, -1), (-1, 1), (-1, -1))
DIRS = SIDES + CORNERS
HI = lax.Precision.HIGHEST
WEIGHT = 0.8 / 0.65


def up(v, axis):
    return pltpu.roll(v, v.shape[axis] - 1, axis)


def down(v, axis):
    return pltpu.roll(v, 1, axis)


def kernel(
    px, py, vel, sta, sol, res, dirn, IMG, PR, o_sc, KEEP,
    F, FV, FC, S, T, U, G, CB, AR,
    loc_sem, h_send, h_recv, s_send, s_recv, u_send, u_recv, c_send, c_recv, a_send, a_recv,
):
    nx, ny, nz = sta.shape[1:]
    ex, ey = nx + 2 * W, ny + 2 * W
    me_x, me_y = lax.axis_index("px"), lax.axis_index("py")

    def at(dx, dy):
        return (lax.rem(me_x + (dx + px), px), lax.rem(me_y + (dy + py), py))

    def mesh_copy(src, dst, s, r, dx, dy):
        return pltpu.make_async_remote_copy(
            src_ref=src, dst_ref=dst, send_sem=s, recv_sem=r,
            device_id=at(dx, dy), device_id_type=pl.DeviceIdType.MESH,
        )

    locals_ = []
    for g, a in enumerate((sta, dirn, vel)):
        locals_.append(
            pltpu.make_async_copy(a, F.at[pl.ds(3 * g, 3), pl.ds(W, nx), pl.ds(0, ny)], loc_sem.at[g])
        )
    for i, a in enumerate((res, dirn, sol)):
        locals_.append(pltpu.make_async_copy(a, KEEP.at[i], loc_sem.at[3 + i]))
    RS = KEEP.at[0]

    barrier = pltpu.get_barrier_semaphore()
    total = px * py

    def peer(d):
        other = lax.rem(me_x * py + me_y + d, total)
        return (other // py, lax.rem(other, py))

    def each_peer(body):
        def run(i, carry):
            body(i + 1)
            return carry

        lax.fori_loop(0, total - 1, run, 0, unroll=total <= 64)

    small = max(px // 2 - 3, 0) + max(py // 2 - 3, 0) <= 2
    if small:
        for dx, dy in SIDES:
            pl.semaphore_signal(barrier, inc=1, device_id=at(dx, dy), device_id_type=pl.DeviceIdType.MESH)
    else:
        each_peer(
            lambda d: pl.semaphore_signal(
                barrier, inc=1, device_id=peer(d), device_id_type=pl.DeviceIdType.MESH
            )
        )
    for c in locals_:
        c.start()
    pl.semaphore_wait(barrier, len(SIDES) if small else total - 1)

    def x_span(dx, w, k):
        return {
            0: (0, nx, W),
            1: (nx - w - k, w, W - w - k),
            -1: (k, w, W + nx + k),
        }[dx]

    def y_span(dy, w, k):
        return {
            0: (0, ny, 0),
            1: (ny - w - k, w, ny + 2 * W - w - k),
            -1: (k, w, ny + k),
        }[dy]

    def halo(make, send, recv, dirs, width, base=0):
        copies = []
        for i, (dx, dy) in enumerate(dirs):
            sx, lx, tx = x_span(dx, width, base)
            sy, ly, ty = y_span(dy, width, base)
            src, dst = make((pl.ds(sx, lx), pl.ds(sy, ly)), (pl.ds(tx, lx), pl.ds(ty, ly)))
            copies.append(mesh_copy(src, dst, send.at[i], recv.at[i], dx, dy))
        return copies

    def launch(copies):
        for c in copies:
            c.start()
        return copies

    def own(g, src):
        return F.at[pl.ds(3 * g, 3), pl.ds(W + src[0].start, src[0].size), src[1]]

    def field_halo(g, slot, *args):
        return halo(
            lambda src, dst: (own(g, src), F.at[(pl.ds(3 * g, 3),) + dst]),
            h_send.at[slot], h_recv.at[slot], *args,
        )

    locals_[0].wait()
    state_copies = launch(field_halo(0, 0, SIDES, 1))
    locals_[2].wait()
    near_copies = launch(field_halo(2, 1, SIDES, 2))

    row = lambda shape: lax.broadcasted_iota(jnp.int32, shape, 0)
    lane = lambda shape: lax.broadcasted_iota(jnp.int32, shape, 1)
    cz = nz // 4
    cx, cy = nx // 4, ny // 4
    lanes = cy * cz
    m_shape = (nz, lanes)
    gather_z = (row(m_shape) // 4 == lax.rem(lane(m_shape), cz)).astype(jnp.float32).astype(jnp.bfloat16)
    t_shape = (lanes, nz)
    spread_z = (lax.rem(row(t_shape), cz) == lane(t_shape) // 4).astype(jnp.float32).astype(jnp.bfloat16)
    own_y = row((ny, lanes)) // 4 == lane((ny, lanes)) // cz
    def sweep(start, planes, step, body):
        def run(i, carry):
            body(start + i * step)
            return carry

        lax.fori_loop(0, planes // step, run, 0, unroll=True)

    def two_terms(v, exact):
        high = v.astype(jnp.bfloat16)
        low = (v - high.astype(jnp.float32)).astype(jnp.bfloat16)
        return sum(jnp.dot(part, exact, preferred_element_type=jnp.float32) for part in (low, high))

    def restrict(read, first):
        x_sums = jnp.concatenate(
            [jnp.sum(read(c, pl.ds(4 * b, 4)), axis=0) for c in range(3) for b in range(cx)], axis=0
        )
        z_sums = two_terms(x_sums, gather_z)
        for c in range(3):
            for b in range(cx):
                at = (c * cx + b) * ny
                block = jnp.where(own_y, z_sums[at : at + ny], 0.0)
                CB[1, 1, b, pl.ds(first + c, 1)] = jnp.sum(block, axis=0, keepdims=True) * (1.0 / 64.0)

    def coarse_halo(first, slot):
        copies = []
        for i, (dx, dy) in enumerate(CORNERS + SIDES):
            xs = {0: pl.ds(0, cx), 1: pl.ds(cx - 3, 3), -1: pl.ds(0, 3)}[dx]
            rows = pl.ds(first, 3)
            c = mesh_copy(
                CB.at[1, 1, xs, rows], CB.at[1 - dx, 1 - dy, xs, rows],
                c_send.at[slot, i], c_recv.at[slot, i], dx, dy,
            )
            copies.append(c)
        return launch(copies)

    locals_[3].wait()
    rr = jnp.zeros((ny, nz), jnp.float32)
    for c in range(3):
        for b in range(cx):
            r = RS[c, pl.ds(4 * b, 4)]
            rr = rr + jnp.sum(r * r, axis=0)
    restrict(lambda c, at: RS[c, at], 0)

    locals_[1].wait()
    for c in state_copies:
        c.wait()

    def gradient(n, x):
        f = F[n, pl.ds(x, 2)]
        return (
            (F[n, pl.ds(x + 1, 2)] - F[n, pl.ds(x - 1, 2)])[:, :ny],
            (up(f, 1) - down(f, 1))[:, :ny],
            (up(f, 2) - down(f, 2))[:, :ny],
        )

    def sources(moments):
        def body(x):
            own = pl.ds(x, 2)
            d = [F[3 + k, own, pl.ds(0, ny)] for k in range(3)]
            for n in moments:
                grads = gradient(n, x)
                S[n, own, pl.ds(0, ny)] = 0.5 * (d[0] * grads[0] + d[1] * grads[1] + d[2] * grads[2])
                for k in range(3):
                    G[3 * n + k, pl.ds(x - W, 2)] = grads[k]

        return body

    sweep(W, nx, 2, sources((0, 1)))
    def source_halo(lo, n, slot, dirs, width):
        return halo(
            lambda src, dst: (
                S.at[pl.ds(lo, n), pl.ds(W + src[0].start, src[0].size), src[1]],
                S.at[(pl.ds(lo, n),) + dst],
            ),
            s_send.at[slot], s_recv.at[slot], dirs, width,
        )

    source_copies = launch(
        source_halo(0, 2, 0, CORNERS, 2)
        + field_halo(2, 4, CORNERS, 1)
        + source_halo(0, 1, 1, SIDES, 3)
        + source_halo(1, 1, 2, SIDES, 2)
    )
    far_copies = halo(
        lambda src, dst: (
            own(2, src),
            FV.at[pl.ds(0, 3), pl.ds(0, nx), pl.ds(dst[1].start - ny, 2)]
            if dst[1].size == 2
            else F.at[(pl.ds(6, 3),) + dst],
        ),
        h_send.at[2], h_recv.at[2], SIDES, 2, 2,
    )
    far_copies += halo(
        lambda src, dst: (
            own(2, src),
            FC.at[pl.ds(0, 3), int(dst[0].start > W), pl.ds(0, 3), pl.ds(dst[1].start - ny, 3)],
        ),
        h_send.at[5], h_recv.at[5], CORNERS, 3,
    )
    far_copies = launch(far_copies)
    direction_copies = launch(field_halo(1, 3, SIDES, 1))
    residual_coarse_copies = coarse_halo(0, 0)
    sweep(W, nx, 2, sources((2,)))

    for c in near_copies:
        c.wait()
    for c in source_copies:
        c.wait()

    def advect(read, x):
        f = read(x)
        v = [F[6 + k, pl.ds(x, 2)] for k in range(3)]
        return f, 0.5 * (
            v[0] * (read(x + 1) - read(x - 1))
            + v[1] * (up(f, 1) - down(f, 1))
            + v[2] * (up(f, 2) - down(f, 2))
        )

    def forward_one(x):
        f, adv = advect(lambda i: S[0, pl.ds(i, 2)], x)
        at_x = pl.ds(x, 2)
        T[1, at_x] = 0.25 * (0.5 * adv - S[1, at_x] - f)

    def forward_two(x):
        f, adv = advect(lambda i: T[1, pl.ds(i, 2)], x)
        at_x = pl.ds(x, 2)
        first = -(adv + S[1, at_x])
        T[2, at_x] = f + 0.5 * first
        T[3, at_x] = f + 0.25 * first

    def forward_three(x):
        f, adv = advect(lambda i: T[2, pl.ds(i, 2)], x)
        at_x = pl.ds(x, 2)
        U[at_x, pl.ds(0, ny)] = 0.25 * (adv[:, :ny] + S[2, at_x, pl.ds(0, ny)]) - T[3, at_x, pl.ds(0, ny)]

    sweep(2, ex - 4, 2, forward_one)
    sweep(3, ex - 6, 2, forward_two)
    sweep(4, ex - 8, 2, forward_three)

    def u_halo(slot, dirs, width):
        return halo(
            lambda src, dst: (U.at[pl.ds(W + src[0].start, src[0].size), src[1]], U.at[dst]),
            u_send.at[slot], u_recv.at[slot], dirs, width,
        )

    u_copies = launch(u_halo(0, CORNERS, 3) + u_halo(1, SIDES, W))
    for c in direction_copies:
        c.wait()

    def base(x):
        own = pl.ds(x, 2)
        at_x = pl.ds(x - W, 2)
        adj = 0.125 * U[own, pl.ds(0, ny)]
        for k in range(3):
            f = F[3 + k, own]
            neighbours = (
                F[3 + k, pl.ds(x + 1, 2)] + F[3 + k, pl.ds(x - 1, 2)]
                + up(f, 1) + down(f, 1) + up(f, 2) + down(f, 2)
            )[:, :ny]
            IMG[k, at_x] = 4.0 * f[:, :ny] - 0.5 * neighbours + adj * G[6 + k, at_x]

    sweep(W, nx, 2, base)
    for c in far_copies:
        c.wait()
    tile_row = lax.broadcasted_iota(jnp.int32, (1, 1, 2 * W, nz), 2)
    band, beyond = pl.ds(W, nx), pl.ds(ny, 2 * W)
    from_far = jnp.logical_and(tile_row >= 2, tile_row < 2 * W - 2)
    F[pl.ds(6, 3), band, beyond] = jnp.where(from_far, FV[...], F[pl.ds(6, 3), band, beyond])
    F[pl.ds(6, 3), pl.ds(W - 3, 3), beyond] = FC[:, 0]
    F[pl.ds(6, 3), pl.ds(W + nx, 3), beyond] = FC[:, 1]
    for c in u_copies:
        c.wait()

    def diverge(read, x):
        f = read(x)
        flux_y = f * F[7, pl.ds(x, 2)]
        flux_z = f * F[8, pl.ds(x, 2)]
        return f, 0.5 * (
            read(x + 1) * F[6, pl.ds(x + 1, 2)]
            - read(x - 1) * F[6, pl.ds(x - 1, 2)]
            + (up(flux_y, 1) - down(flux_y, 1))
            + (up(flux_z, 2) - down(flux_z, 2))
        )

    def adjoint_first(read):
        def body(x):
            f, rate = diverge(read, x)
            at_x = pl.ds(x, 2)
            T[0, at_x] = f + 0.5 * rate
            T[1, at_x] = f + 0.25 * rate

        return body

    def adjoint_second(x):
        f, rate = diverge(lambda i: T[0, pl.ds(i, 2)], x)
        at_x = pl.ds(x, 2)
        T[2, at_x] = T[1, at_x] + 0.25 * rate

    def adjoint_last(x):
        f, rate = diverge(lambda i: T[0, pl.ds(i, 2)], x)
        own = pl.ds(x, 2)
        at_x = pl.ds(x - W, 2)
        adj_zero = 0.125 * (T[1, own] + 0.25 * rate)[:, :ny]
        adj_one = 0.25 * T[2, own, pl.ds(0, ny)]
        for k in range(3):
            IMG[k, at_x] = IMG[k, at_x] + adj_one * G[3 + k, at_x] + adj_zero * G[k, at_x]

    sweep(1, ex - 2, 2, adjoint_first(lambda i: U[pl.ds(i, 2)]))
    sweep(2, ex - 4, 2, adjoint_second)
    sweep(3, ex - 6, 2, adjoint_first(lambda i: T[2, pl.ds(i, 2)]))
    sweep(4, ex - 8, 2, adjoint_last)

    restrict(lambda c, at: IMG[c, at], 3)
    c_copies = residual_coarse_copies + coarse_halo(3, 1)

    rq = jnp.zeros((ny, nz), jnp.float32)
    qq = jnp.zeros((ny, nz), jnp.float32)
    dq = jnp.zeros((ny, nz), jnp.float32)
    for c in range(3):
        for b in range(cx):
            q = IMG[c, pl.ds(4 * b, 4)]
            rq = rq + jnp.sum(q * RS[c, pl.ds(4 * b, 4)], axis=0)
            qq = qq + jnp.sum(q * q, axis=0)
            dq = dq + jnp.sum(q * F[3 + c, pl.ds(W + 4 * b, 4)][:, :ny], axis=0)
    flat = lambda v: jnp.sum(v, axis=0, keepdims=True)
    rr, rq, qq, dq = flat(rr), flat(rq), flat(qq), flat(dq)

    for c in c_copies:
        c.wait()
    b_all = jnp.concatenate(
        [jnp.concatenate([CB[a, e] for e in range(3)], axis=2) for a in range(3)], axis=0
    )
    b_all = b_all[cx - 3 : 2 * cx + 3]
    z_pos = lax.rem(lax.broadcasted_iota(jnp.int32, (1, 8, 3 * lanes), 2), cz)
    total_lanes = 3 * lanes
    approx = WEIGHT * b_all
    for turn in range(3):
        mid = approx[1:-1]
        z_up = jnp.where(z_pos == cz - 1, pltpu.roll(mid, cz - 1, 2), pltpu.roll(mid, total_lanes - 1, 2))
        z_down = jnp.where(z_pos == 0, pltpu.roll(mid, total_lanes - cz + 1, 2), pltpu.roll(mid, 1, 2))
        around = (
            approx[2:] + approx[:-2]
            + pltpu.roll(mid, cz, 2) + pltpu.roll(mid, total_lanes - cz, 2)
            + z_up + z_down
        )
        approx = 0.2 * mid + WEIGHT * (b_all[turn + 1 : -turn - 1] + 0.1 * around)
    r8 = row((8, lanes))
    e = jnp.where(r8[None] < 6, approx[:, :, lanes : 2 * lanes], 0.0)
    b_own = CB[1, 1]
    same = jnp.sum(b_own * e, axis=0)
    cross = jnp.sum(b_own * jnp.where(r8[None] < 3, pltpu.roll(e, 5, 1), pltpu.roll(e, 3, 1)), axis=0)
    pick = lambda v, lo, hi: flat(jnp.where(jnp.logical_and(r8 >= lo, r8 < hi), v, 0.0))
    sum_a = 0.25 * rr + 64.0 * pick(same, 0, 3)
    sum_b = 0.5 * rq + 64.0 * pick(cross, 0, 6)
    sum_c = 0.25 * qq + 64.0 * pick(same, 3, 6)
    def folded(v):
        v = v + pltpu.roll(v, lanes // 2, 1)
        return v + pltpu.roll(v, lanes // 4, 1)

    quarter = lane((1, lanes)) // (lanes // 4)
    AR[0] = jnp.where(
        quarter < 2,
        jnp.where(quarter == 0, folded(sum_a), folded(sum_b)),
        jnp.where(quarter == 2, folded(sum_c), folded(dq)),
    )

    around_x = [lax.rem(me_x + i, px) for i in range(px)]
    around_y = [lax.rem(me_y + j, py) for j in range(py)]

    def sums_copy(d):
        other = (around_x[d // py], around_y[d % py]) if isinstance(d, int) else peer(d)
        return pltpu.make_async_remote_copy(
            src_ref=AR.at[0], dst_ref=AR.at[d], send_sem=a_send.at[d], recv_sem=a_recv.at[d],
            device_id=other, device_id_type=pl.DeviceIdType.MESH,
        )

    if total <= 64:
        far_y = sorted(range(py), key=lambda j: -abs(2 * j - py) if j else 1)
        far_x = sorted(range(px), key=lambda i: abs(2 * i - px))
        order = [i * py + j for j in far_y for i in far_x if i or j]
        for d in order:
            sums_copy(d).start()
    else:
        each_peer(lambda d: sums_copy(d).start())

    wide = jnp.concatenate(
        [jnp.where(own_y, e[b, c : c + 1], 0.0) for c in range(6) for b in range(cx)], axis=0
    )
    PR[...] = two_terms(wide, spread_z).reshape(6, cx, ny, nz)

    if total <= 64:
        for d in range(1, total):
            sums_copy(d).wait()
    else:
        each_peer(lambda d: sums_copy(d).wait())
    sums = jnp.sum(AR[...], axis=0)
    rz, mixed, square, curvature = (
        jnp.sum(jnp.where(quarter == i, sums, 0.0), axis=1, keepdims=True) for i in range(4)
    )
    alpha = rz / curvature
    beta = (rz - alpha * mixed + alpha * alpha * square) / rz
    o_sc[...] = jnp.where(r8 == 0, alpha, beta)
    for c in locals_[4:]:
        c.wait()


def finish(scalars, coarse, image, keep, o_sol, o_res, o_dir, N, sem):
    alpha, beta = scalars[0:1, 0:1].reshape(1, 1, 1), scalars[1:2, 0:1].reshape(1, 1, 1)
    copies = []
    for c in range(3):
        for b in range(coarse.shape[1]):
            at_x = pl.ds(4 * b, 4)
            d = keep[1, c, at_x]
            left = keep[0, c, at_x] - alpha * image[c, at_x]
            mixed = coarse[c, pl.ds(b, 1)] - alpha * coarse[3 + c, pl.ds(b, 1)]
            N[0, c, at_x] = keep[2, c, at_x] + alpha * d
            N[1, c, at_x] = left
            N[2, c, at_x] = 0.25 * left + mixed + beta * d
        for i, out in enumerate((o_sol, o_res, o_dir)):
            copy = pltpu.make_async_copy(N.at[i, c], out.at[c], sem.at[3 * i + c])
            copy.start()
            copies.append(copy)
    for copy in copies:
        copy.wait()


def solution(mesh):
    px, py = mesh.shape["px"], mesh.shape["py"]
    spec = P(None, "px", "py", None)

    def local(velocity, states, solution, residual, direction):
        comps, nx, ny, nz = velocity.shape
        ex, ey = nx + 2 * W, ny + 2 * W
        cx = nx // 4
        lanes = (ny // 4) * (nz // 4)
        f32 = jnp.float32
        dma = pltpu.SemaphoreType.DMA
        shape = jax.ShapeDtypeStruct
        anywhere = pl.BlockSpec(memory_space=pl.ANY)
        vmem = pl.BlockSpec(memory_space=pltpu.VMEM)
        image, spread, scalars, keep = pl.pallas_call(
                functools.partial(kernel, px, py),
                out_shape=[
                    shape(velocity.shape, f32), shape((6, cx, ny, nz), f32), shape((8, lanes), f32),
                    shape((3,) + velocity.shape, f32),
                ],
                in_specs=[anywhere] * 5,
                out_specs=[vmem] * 4,
                scratch_shapes=[
                    pltpu.VMEM((9, ex, ey, nz), f32),
                    pltpu.VMEM((3, nx, 2 * W, nz), f32),
                    pltpu.VMEM((3, 2, 3, 2 * W, nz), f32),
                    pltpu.VMEM((3, ex, ey, nz), f32),
                    pltpu.VMEM((4, ex, ey, nz), f32),
                    pltpu.VMEM((ex, ey, nz), f32),
                    pltpu.VMEM((9, nx, ny, nz), f32),
                    pltpu.VMEM((3, 3, cx, 8, lanes), f32),
                    pltpu.VMEM((px * py, 1, lanes), f32),
                    dma((6,)),
                    dma((6, 4)),
                    dma((6, 4)),
                    dma((3, 4)),
                    dma((3, 4)),
                    dma((2, 4)),
                    dma((2, 4)),
                    dma((2, 8)),
                    dma((2, 8)),
                    dma((px * py,)),
                    dma((px * py,)),
                ],
                compiler_params=pltpu.CompilerParams(
                    collective_id=0, has_side_effects=True, vmem_limit_bytes=24 * 2**20
                ),
            )(*(pltpu.with_memory_space_constraint(a, pltpu.HBM) for a in (velocity, states, solution, residual, direction)))
        return tuple(
            pl.pallas_call(
                finish,
                out_shape=[shape(velocity.shape, f32)] * 3,
                in_specs=[vmem] * 4,
                out_specs=[anywhere] * 3,
                scratch_shapes=[pltpu.VMEM((3,) + velocity.shape, f32), dma((9,))],
                compiler_params=pltpu.CompilerParams(vmem_limit_bytes=8 * 2**20),
            )(scalars, spread, image, keep)
        )

    return jax.shard_map(local, mesh=mesh, in_specs=(spec,) * 5, out_specs=(spec,) * 3, check_vma=False)
```
